128 devices in a mesh: ctx: 32 (over x, y, core), tp: 4 (over z).
Axes of the slice: x: 4, y: 4, z: 4, core: 2. Of those that a mesh axis runs over, the one named last changes fastest.
Arguments:
- queries: bfloat16 [512, 8192], P('ctx', 'tp'), may hold values from -60 to 60
- rotated_keys: bfloat16 [4096, 1024], P('ctx', 'tp'), may hold values from -7 to 7
- value_rows: bfloat16 [4096, 1024], P('ctx', 'tp'), may hold values from -6 to 6
- span_order: int32 [64], replicated, may hold values from 0 to 63, each once
- targets: int32 [512], replicated, may hold values from 0 to 65535
- out_weight: bfloat16 [8192, 4, 32, 64], P('tp', None, 'ctx'), may hold values from -0.0625 to 0.0625
- residual: bfloat16 [512, 4, 32, 64], P(None, 'tp', 'ctx'), may hold values from -3 to 3
- norm_gain: float32 [4, 32, 64], P('tp', 'ctx'), may hold values from 0.5 to 1.5
- head_weight: bfloat16 [8192, 65536], P('tp', 'ctx'), may hold values from -2.253903 to 2.253903
Outputs:
- loss: float32 [], replicated
- grad_normed: bfloat16 [512, 8192], P('ctx', 'tp')
- grad_head: bfloat16 [8192, 65536], P('tp', 'ctx')
The draws below stay inside these ranges and needn't reach their ends.
Inputs may be any that keep to these rules, and one draw needn't show every extreme that they name: `span_order`: each span number appears once.
All inputs are finite; a program needn't handle non-finite values.
Results may differ from the reference program's by a relative error of at most 0.012.
Values may be sent and summed in bfloat16 or wider, within the bound.
No kernel may reach another device: no remote copies, remote signals or barrier semaphores. Data moves between devices by JAX's collectives and lax.ppermute only.
A program may use at most 128 MiB of HBM per device.

```python
import math
import jax
import jax.numpy as jnp
import numpy as np
from jax import lax

D = 8192
QUERY_HEADS = 64
KEY_VALUE_HEADS = 8
HEAD_SIZE = 128
VOCAB = 65536
SPAN = 64
Q_SPAN = 8
SEQUENCE_TOKENS = 4096
QUERY_TOKENS = 512
NSPANS = 64
SLICE = 64
N_CTX = 32
N_TP = 4


def paired_states(key):
    base_key = jax.random.fold_in(key, 907)
    key_layout = (SEQUENCE_TOKENS, KEY_VALUE_HEADS * HEAD_SIZE)
    query_layout = (QUERY_TOKENS, QUERY_HEADS * HEAD_SIZE)
    key_vals = jnp.clip(jax.random.normal(jax.random.fold_in(base_key, 1), key_layout, jnp.float32), -6.0, 6.0)
    query_vals = jnp.clip(jax.random.normal(jax.random.fold_in(base_key, 2), query_layout, jnp.float32), -6.0, 6.0)
    return (query_vals, key_vals)


def draw_queries(key, part):
    return paired_states(key)[0].astype(jnp.bfloat16)


def draw_rotated_keys(key, part):
    return paired_states(key)[1].astype(jnp.bfloat16)


def draw_head_weight(key, part):
    spread = 3.0 * D ** (-0.5)
    normal_vals = jnp.clip(jax.random.normal(jax.random.fold_in(key, 11), (D, VOCAB), jnp.float32), -6.0, 6.0)
    return (normal_vals * spread).astype(jnp.bfloat16)


def touch_ends(entries, stream_key, low, largest):
    spot = [jax.random.randint(jax.random.fold_in(stream_key, axis), (), 0, length) for axis, length in enumerate(entries.shape)]
    widest = entries.shape.index(max(entries.shape))
    next_to = spot[:widest] + [(spot[widest] + 1) % entries.shape[widest]] + spot[widest + 1:]
    return entries.at[tuple(spot)].set(low).at[tuple(next_to)].set(largest)


def levels(key, dims, cuts, smallest, high):
    level, own = 1.0, jax.random.fold_in(key, 6)
    for dim, parts in cuts:
        steps = jnp.exp(jax.random.uniform(jax.random.fold_in(own, dim), (parts,), jnp.float32, smallest / len(cuts), high / len(cuts)))
        level = level * jnp.repeat(steps, dims[dim] // parts).reshape([-1 if axis == dim else 1 for axis in range(len(dims))])
    return level


def cumulative_ranks(amount, slope):
    loads = [(1 << 20) // math.isqrt(standing ** slope) + 1 for standing in range(1, amount + 1)]
    deviation = 1 + sum(loads) // (1 << 30)
    return np.cumsum(np.array([max(1, weight // deviation) for weight in loads]))


def ranked(own_key, shape, amount, lean):
    table = cumulative_ranks(amount, lean)
    pick = jax.random.randint(jax.random.fold_in(own_key, 1), shape, 0, int(table[amount - 1]))
    rank = jnp.searchsorted(jnp.asarray(table, jnp.int32), pick, side="right")
    return jax.random.permutation(jax.random.fold_in(own_key, 2), amount)[rank].astype(jnp.int32)


def bell_draw(key, shape, scale, reach, cuts=(), kind=jnp.bfloat16):
    gain = levels(key, shape, cuts, -0.22, 0.18) if cuts else 1.0
    drawn = jax.random.normal(key, shape, jnp.float32) * scale * gain
    return jnp.minimum(jnp.maximum(drawn, -reach), reach).astype(kind)


def setup_inputs(seed: int = 0) -> dict:
    arg_keys = jax.random.split(jax.random.key(seed), 10)
    return {
        "queries": draw_queries(jax.random.fold_in(arg_keys[9], 71), 0),
        "rotated_keys": draw_rotated_keys(jax.random.fold_in(arg_keys[9], 71), 0),
        "value_rows": bell_draw(arg_keys[2], (SEQUENCE_TOKENS, KEY_VALUE_HEADS * HEAD_SIZE), 1.0, 6.0, ((0, 32), (1, 4))),
        "span_order": jax.random.permutation(arg_keys[3], NSPANS).astype(jnp.int32),
        "targets": touch_ends(ranked(arg_keys[4], (QUERY_TOKENS,), VOCAB, 2), jax.random.fold_in(arg_keys[4], 3), 0, VOCAB - 1).astype(jnp.int32),
        "out_weight": bell_draw(arg_keys[5], (QUERY_HEADS * HEAD_SIZE, N_TP, N_CTX, SLICE), (QUERY_HEADS * HEAD_SIZE) ** -0.5, 0.0625, ((0, 4), (2, 32))),
        "residual": bell_draw(arg_keys[6], (QUERY_TOKENS, N_TP, N_CTX, SLICE), 0.5, 3.0, ((1, 4), (2, 32))),
        "norm_gain": jnp.clip(1.0 + 0.1 * jax.random.normal(arg_keys[7], (N_TP, N_CTX, SLICE), jnp.float32), 0.5, 1.5),
        "head_weight": draw_head_weight(jax.random.fold_in(arg_keys[9], 71), 0),
    }


EPSILON = 1e-05
MASKED = -1e+30

def key_positions(span_order):
    slots = jnp.arange(SEQUENCE_TOKENS, dtype=jnp.int32)
    return span_order[slots // SPAN].astype(jnp.int32) * SPAN + slots % SPAN

def query_positions(span_order):
    slots = jnp.arange(QUERY_TOKENS, dtype=jnp.int32)
    return span_order[slots // Q_SPAN].astype(jnp.int32) * SPAN + (SPAN - Q_SPAN) + slots % Q_SPAN

def reference(queries, rotated_keys, value_rows, span_order, targets, out_weight, residual, norm_gain, head_weight):
    key_pos = key_positions(span_order)
    query_pos = query_positions(span_order)
    visible = key_pos[None, :] <= query_pos[:, None]
    group_size = QUERY_HEADS // KEY_VALUE_HEADS
    grouped_queries = queries.astype(jnp.float32).reshape(QUERY_TOKENS, KEY_VALUE_HEADS, group_size, HEAD_SIZE).transpose(1, 0, 2, 3)
    divided_keys = rotated_keys.astype(jnp.float32).reshape(SEQUENCE_TOKENS, KEY_VALUE_HEADS, HEAD_SIZE).transpose(1, 0, 2)
    divided_values = value_rows.astype(jnp.float32).reshape(SEQUENCE_TOKENS, KEY_VALUE_HEADS, HEAD_SIZE).transpose(1, 0, 2)

    def one_head(inputs):
        head_q, head_k, head_v = inputs
        scores = jnp.einsum('tgd,sd->gts', head_q, head_k) * HEAD_SIZE ** (-0.5)
        scores = jnp.where(visible[None], scores, MASKED)
        peak = lax.optimization_barrier(jnp.max(scores, axis=-1, keepdims=True))
        expo = jnp.exp(scores - peak)
        weights = (expo / lax.optimization_barrier(jnp.sum(expo, axis=-1, keepdims=True))).astype(jnp.bfloat16)
        weights = lax.optimization_barrier(weights).astype(jnp.float32)
        return jnp.einsum('gts,sd->tgd', weights, head_v).astype(jnp.bfloat16)
    heads_out = lax.map(one_head, (grouped_queries, divided_keys, divided_values))
    attn = heads_out.transpose(1, 0, 2, 3).reshape(QUERY_TOKENS, QUERY_HEADS * HEAD_SIZE)
    projected = jnp.dot(attn, out_weight.reshape(QUERY_HEADS * HEAD_SIZE, D), preferred_element_type=jnp.float32)
    hidden = residual.reshape(QUERY_TOKENS, D).astype(jnp.float32) + projected
    mean_sq = lax.optimization_barrier(jnp.mean(hidden * hidden, axis=1))
    normed = (hidden * lax.rsqrt(mean_sq + EPSILON)[:, None] * norm_gain.reshape(D)).astype(jnp.bfloat16)
    logits = jnp.dot(normed, head_weight, preferred_element_type=jnp.float32)
    peak = lax.optimization_barrier(jnp.max(logits, axis=1))
    lse = peak + jnp.log(lax.optimization_barrier(jnp.sum(jnp.exp(logits - peak[:, None]), axis=1)))
    picked = jnp.take_along_axis(logits, targets[:, None].astype(jnp.int32), axis=1)[:, 0]
    loss = jnp.mean(lse - picked)
    target_hit = jnp.arange(VOCAB, dtype=jnp.int32)[None, :] == targets[:, None]
    grad_logits = (jnp.exp(logits - lse[:, None]) - target_hit.astype(jnp.float32)).astype(jnp.bfloat16)
    grad_normed = jnp.dot(grad_logits, head_weight.T, preferred_element_type=jnp.float32).astype(jnp.bfloat16)
    grad_head = jnp.dot(normed.T, grad_logits, preferred_element_type=jnp.float32).astype(jnp.bfloat16)
    return (loss, grad_normed, grad_head)
```

```python
import jax
import jax.numpy as jnp
from jax import lax
from jax.sharding import Mesh
from jax.sharding import PartitionSpec as P

D = 8192
KEY_VALUE_HEADS = 8
HEAD_SIZE = 128

EPSILON = 1e-05
MASKED = -1e30

NX, NY, NC, NZ = 4, 4, 2, 4
CTX = ("x", "y", "c")
PLANE = ("x", "y")
CHIPS = ("x", "y", "z")
F32 = jnp.float32
BF16 = jnp.bfloat16
F16 = jnp.float16


def swap(value):
    return lax.ppermute(value, "c", [(0, 1), (1, 0)])


def exchange(value, axes):
    return lax.all_to_all(value, axes, 0, 0, tiled=True)


def spread(value, axes, count):
    copies = jnp.broadcast_to(value[None], (count,) + value.shape)
    return lax.all_to_all(copies, axes, 0, 0, tiled=True)


def pick(pair, index):
    return lax.dynamic_index_in_dim(pair, index, 0, keepdims=False)


def span_starts(span_order, repeat, span_rows):
    return jnp.repeat(span_order * span_rows, repeat, total_repeat_length=span_order.shape[0] * repeat)


def attend(grouped, keys, values, visible):
    scores = lax.dot_general(
        grouped, keys, (((1,), (1,)), ((), ())), preferred_element_type=F32
    ) * HEAD_SIZE ** (-0.5)
    scores = jnp.where(visible, scores, MASKED)
    peak = jnp.max(scores, axis=-1, keepdims=True)
    expo = jnp.exp(scores - peak)
    weights = (expo / jnp.sum(expo, axis=-1, keepdims=True)).astype(BF16)
    return jnp.dot(weights, values, preferred_element_type=F32).astype(BF16)


def per_device(
    queries,
    rotated_keys,
    value_rows,
    span_order,
    targets,
    out_weight,
    residual,
    norm_gain,
    head_weight,
):
    x, y, c, z = (lax.axis_index(a) for a in ("x", "y", "c", "z"))
    xy = x * NY + y
    first = c == 0
    q_dev = queries.shape[0]
    tok_dev = rotated_keys.shape[0]
    planes = NX * NY
    span_rows = tok_dev // 2
    q_span = q_dev // 2
    total_rows = q_dev * planes * NC
    total_keys = tok_dev * planes * NC
    half_rows = total_rows // NC

    key_pair = rotated_keys.reshape(tok_dev, NC, HEAD_SIZE).transpose(1, 0, 2)
    value_pair = value_rows.reshape(tok_dev, NC, HEAD_SIZE).transpose(1, 0, 2)
    packed = jnp.concatenate([key_pair, value_pair], axis=2)
    packed = jnp.broadcast_to(packed[None], (planes,) + packed.shape)
    gathered = exchange(packed.reshape(planes * NC, tok_dev, 2 * HEAD_SIZE), CTX)
    gathered = gathered.reshape(total_keys, 2 * HEAD_SIZE)
    keys, values = gathered[:, :HEAD_SIZE], gathered[:, HEAD_SIZE:]

    head_width = queries.shape[1] // NC
    query_pair = queries.reshape(q_dev, NC, head_width).transpose(1, 0, 2)
    q_own = pick(query_pair, c)
    q_got = swap(pick(query_pair, 1 - c))
    chip_queries = jnp.where(
        first, jnp.concatenate([q_own, q_got]), jnp.concatenate([q_got, q_own])
    )
    chip_rows = 2 * q_dev
    group = head_width // HEAD_SIZE
    grouped = (
        chip_queries.reshape(chip_rows, group, HEAD_SIZE)
        .transpose(1, 0, 2)
        .reshape(group * chip_rows, HEAD_SIZE)
    )

    slice_width = out_weight.shape[3]
    out_pair = out_weight.reshape(NC, out_weight.shape[0] // NC, NZ, slice_width)
    out_own = pick(out_pair, c)
    out_got = swap(pick(out_pair, 1 - c))
    out_low = jnp.where(first, out_own, out_got)
    out_high = jnp.where(first, out_got, out_own)
    out_both = jnp.stack([out_low, out_high], axis=2).reshape(-1, NZ * NC * slice_width)
    gain_own = norm_gain.reshape(slice_width)
    gain_got = swap(gain_own)
    gain = jnp.concatenate(
        [jnp.where(first, gain_own, gain_got), jnp.where(first, gain_got, gain_own)]
    )
    head_got = swap(head_weight)

    key_pos = span_starts(span_order, span_rows, span_rows) + jnp.arange(total_keys) % span_rows
    query_pos = (
        span_starts(span_order, q_span, span_rows)
        + (span_rows - q_span)
        + jnp.arange(total_rows) % q_span
    )
    chip_pos = lax.dynamic_slice_in_dim(query_pos, xy * chip_rows, chip_rows)
    row_pos = jnp.broadcast_to(chip_pos[None], (group, chip_rows)).reshape(-1)
    visible = key_pos[None, :] <= row_pos[:, None]
    attn = attend(grouped, keys, values, visible)
    attn = attn.reshape(group, chip_rows, HEAD_SIZE).transpose(1, 0, 2).reshape(chip_rows, -1)
    attn_all = spread(attn, PLANE, planes).reshape(total_rows, -1)

    mixed = jnp.dot(attn_all, out_both, preferred_element_type=F32)
    mine = (jnp.arange(NZ)[:, None] == z) & (jnp.arange(NC)[None, :] == c)
    own_part = jnp.where(
        mine[None, :, :, None],
        residual.reshape(total_rows, 1, 1, slice_width).astype(F32),
        0.0,
    ).reshape(total_rows, -1)
    mixed = mixed + own_part
    mixed_pair = mixed.reshape(planes, NC, q_dev, -1).transpose(1, 0, 2, 3)
    mixed = pick(mixed_pair, c) + swap(pick(mixed_pair, 1 - c))
    width = NC * slice_width
    mixed = mixed.reshape(half_rows, NZ, width).transpose(1, 0, 2)
    hidden = jnp.sum(exchange(mixed, "z"), axis=0)

    square_part = jnp.sum(hidden * hidden, axis=1).reshape(-1, 128)
    squares = jnp.sum(spread(square_part, CHIPS, planes * NZ).reshape(planes * NZ, half_rows), axis=0)
    normed = (hidden * lax.rsqrt(squares / D + EPSILON)[:, None] * gain[None, :]).astype(BF16)
    block = (
        spread(normed, PLANE, planes)
        .reshape(planes, half_rows, width)
        .transpose(1, 0, 2)
        .reshape(half_rows, -1)
    )
    block_got = swap(block)

    vocab_width = head_weight.shape[1]
    z_rows = half_rows // NZ

    def summed_logits(weight):
        part = jnp.dot(block, weight, preferred_element_type=F32).astype(F16)
        parts = exchange(part, "z").reshape(NZ, z_rows, vocab_width)
        return jnp.sum(parts.astype(F32), axis=0)

    logits = (summed_logits(head_weight), summed_logits(head_got))
    row_targets = pick(targets.reshape(planes, NC, q_dev).transpose(1, 0, 2), c).reshape(-1)
    row_targets = lax.dynamic_slice_in_dim(row_targets, z * z_rows, z_rows)
    columns = jnp.arange(vocab_width, dtype=jnp.int32)[None, :]
    hits = tuple(
        columns + (xy * NC + core) * vocab_width == row_targets[:, None] for core in (c, 1 - c)
    )
    peak = jnp.maximum(jnp.max(logits[0], axis=1), jnp.max(logits[1], axis=1))
    total = sum(jnp.sum(jnp.exp(part - peak[:, None]), axis=1) for part in logits)
    picked = sum(
        jnp.sum(jnp.where(hit, part, 0.0), axis=1) for hit, part in zip(hits, logits)
    )
    stats = jnp.pad(jnp.stack([peak, total, picked]), ((0, 5), (0, 128 - z_rows)))
    stats = spread(stats, CHIPS, planes * NZ).reshape(planes, NZ, 8, 128)[:, :, :3, :z_rows]
    row_peak = jnp.max(stats[:, :, 0], axis=0)
    row_total = jnp.sum(stats[:, :, 1] * jnp.exp(stats[:, :, 0] - row_peak[None]), axis=0)
    row_lse = row_peak + jnp.log(row_total)
    row_loss = jnp.sum(row_lse - jnp.sum(stats[:, :, 2], axis=0)).reshape(1, 1)
    loss = ((row_loss + swap(row_loss)) / total_rows).reshape(())
    lse = pick(row_lse, z)

    grads = [
        (jnp.exp(part - lse[:, None]) - hit.astype(F32)).astype(BF16)
        for hit, part in zip(hits, logits)
    ]
    grad_own, grad_far = (
        spread(g, "z", NZ).reshape(half_rows, vocab_width) for g in grads
    )
    grad_got = swap(grad_far)
    transposed = (((1,), (1,)), ((), ()))
    grad_rows = lax.dot_general(
        grad_own, head_weight, transposed, preferred_element_type=F32
    ) + lax.dot_general(grad_far, head_got, transposed, preferred_element_type=F32)
    grad_parts = exchange(grad_rows.astype(BF16), PLANE).reshape(planes, q_dev, -1)
    grad_normed = jnp.sum(grad_parts.astype(F32), axis=0).astype(BF16)
    grad_head = lax.dot_general(
        jnp.concatenate([block, block_got]),
        jnp.concatenate([grad_own, grad_got]),
        (((0,), (0,)), ((), ())),
        preferred_element_type=F32,
    ).astype(BF16)
    return (loss, grad_normed, grad_head)


def solution(mesh):
    fine = Mesh(mesh.devices.reshape(NX, NY, NC, NZ), ("x", "y", "c", "z"))
    placed = (
        P(CTX, "z"),
        P(CTX, "z"),
        P(CTX, "z"),
        P(),
        P(),
        P("z", None, CTX, None),
        P(None, "z", CTX, None),
        P("z", CTX, None),
        P("z", CTX),
    )
    return jax.shard_map(
        per_device,
        mesh=fine,
        in_specs=placed,
        out_specs=(P(), P(CTX, "z"), P("z", CTX)),
        check_vma=False,
    )
```

```python
import jax
import jax.numpy as jnp
from jax import lax
from jax.experimental import pallas as pl
from jax.experimental.pallas import tpu as pltpu
from jax.sharding import Mesh
from jax.sharding import PartitionSpec as P

D = 8192
KEY_VALUE_HEADS = 8
HEAD_SIZE = 128

EPSILON = 1e-05
MASKED = -1e30

NX, NY, NC, NZ = 4, 4, 2, 4
CTX = ("x", "y", "c")
PLANE = ("x", "y")
CHIPS = ("x", "y", "z")
F32 = jnp.float32
BF16 = jnp.bfloat16
F16 = jnp.float16


def swap(value):
    return lax.ppermute(value, "c", [(0, 1), (1, 0)])


def exchange(value, axes):
    return lax.all_to_all(value, axes, 0, 0, tiled=True)


def spread(value, axes, count):
    copies = jnp.broadcast_to(value[None], (count,) + value.shape)
    return lax.all_to_all(copies, axes, 0, 0, tiled=True)


def pick(pair, index):
    return lax.dynamic_index_in_dim(pair, index, 0, keepdims=False)


def ring(value, step):
    return lax.ppermute(value, "z", [(i, (i + step) % NZ) for i in range(NZ)])


def rolled(parts, index):
    return [pick(parts, (index + k) % NZ) for k in range(NZ)]


def span_offsets(span_ref, base, count, index, rows):
    starts = jnp.full(index.shape, span_ref[base], jnp.int32)
    for k in range(1, count):
        starts = jnp.where(index >= k * rows, span_ref[base + k], starts)
    return starts


KEY_CHUNK = 512


def attention_body(span_ref, place_ref, query_ref, packed_ref, out_ref, score_ref):
    chip_rows, width = query_ref.shape
    group = width // HEAD_SIZE
    spans = span_ref.shape[0]
    total_keys = packed_ref.shape[0]
    span_rows = total_keys // spans
    chunk_spans = KEY_CHUNK // span_rows
    chip_spans = spans // (NX * NY)
    q_span = chip_rows // chip_spans
    chunks = total_keys // KEY_CHUNK
    rows = group * chip_rows
    query = jnp.concatenate(
        [query_ref[:, g * HEAD_SIZE : (g + 1) * HEAD_SIZE] for g in range(group)], axis=0
    )
    row = lax.broadcasted_iota(jnp.int32, (rows, 1), 0) % chip_rows
    starts = span_offsets(span_ref, place_ref[0] * chip_spans, chip_spans, row, q_span)
    query_pos = starts * span_rows + (span_rows - q_span) + row % q_span
    lane = lax.broadcasted_iota(jnp.int32, (1, KEY_CHUNK), 1)

    def score(i, peak):
        keys = packed_ref[pl.ds(i * KEY_CHUNK, KEY_CHUNK), :HEAD_SIZE]
        scores = lax.dot_general(
            query, keys, (((1,), (1,)), ((), ())), preferred_element_type=F32
        ) * HEAD_SIZE ** (-0.5)
        key_starts = span_offsets(span_ref, i * chunk_spans, chunk_spans, lane, span_rows)
        key_pos = key_starts * span_rows + lane % span_rows
        scores = jnp.where(key_pos <= query_pos, scores, MASKED)
        score_ref[i] = scores
        for k in range(KEY_CHUNK // 128):
            peak = jnp.maximum(peak, scores[:, k * 128 : (k + 1) * 128])
        return peak

    peak = lax.fori_loop(0, chunks, score, jnp.full((rows, 128), MASKED, F32))
    peak = jnp.max(peak, axis=1, keepdims=True)

    def expo(i, total):
        grown = jnp.exp(score_ref[i] - peak)
        score_ref[i] = grown
        for k in range(KEY_CHUNK // 128):
            total = total + grown[:, k * 128 : (k + 1) * 128]
        return total

    total = lax.fori_loop(0, chunks, expo, jnp.zeros((rows, 128), F32))
    inverse = 1.0 / jnp.sum(total, axis=1, keepdims=True)

    def weigh(i, acc):
        weights = (score_ref[i] * inverse).astype(BF16)
        values = packed_ref[pl.ds(i * KEY_CHUNK, KEY_CHUNK), HEAD_SIZE:]
        return acc + jnp.dot(weights, values, preferred_element_type=F32)

    acc = lax.fori_loop(0, chunks, weigh, jnp.zeros((rows, HEAD_SIZE), F32)).astype(BF16)
    for g in range(group):
        out_ref[:, g * HEAD_SIZE : (g + 1) * HEAD_SIZE] = acc[g * chip_rows : (g + 1) * chip_rows]


def attend(span_order, place, query, packed):
    rows = query.shape[0] * query.shape[1] // HEAD_SIZE
    chunks = packed.shape[0] // KEY_CHUNK
    return pl.pallas_call(
        attention_body,
        grid_spec=pltpu.PrefetchScalarGridSpec(
            num_scalar_prefetch=2,
            grid=(1,),
            in_specs=[
                pl.BlockSpec(query.shape, lambda i, s, p: (0, 0)),
                pl.BlockSpec(packed.shape, lambda i, s, p: (0, 0)),
            ],
            out_specs=pl.BlockSpec(query.shape, lambda i, s, p: (0, 0)),
            scratch_shapes=[pltpu.VMEM((chunks, rows, KEY_CHUNK), F32)],
        ),
        out_shape=jax.ShapeDtypeStruct(query.shape, BF16),
        name="attend",
    )(span_order, place, query, packed)


def per_device(
    queries,
    rotated_keys,
    value_rows,
    span_order,
    targets,
    out_weight,
    residual,
    norm_gain,
    head_weight,
):
    x, y, c, z = (lax.axis_index(a) for a in ("x", "y", "c", "z"))
    xy = x * NY + y
    first = c == 0
    q_dev = queries.shape[0]
    tok_dev = rotated_keys.shape[0]
    planes = NX * NY
    total_rows = q_dev * planes * NC
    total_keys = tok_dev * planes * NC
    half_rows = total_rows // NC

    packed = jnp.stack(
        [
            jnp.concatenate(
                [a[:, h * HEAD_SIZE : (h + 1) * HEAD_SIZE] for a in (rotated_keys, value_rows)], axis=1
            )
            for h in range(NC)
        ]
    )
    packed = jnp.broadcast_to(packed[None], (planes,) + packed.shape)
    packed = exchange(packed.reshape(planes * NC, tok_dev, 2 * HEAD_SIZE), CTX)
    packed = packed.reshape(total_keys, 2 * HEAD_SIZE)

    head_width = queries.shape[1] // NC
    q_low, q_high = queries[:, :head_width], queries[:, head_width:]
    q_own = jnp.where(first, q_low, q_high)
    q_got = swap(jnp.where(first, q_high, q_low))
    chip_queries = jnp.concatenate([jnp.where(first, q_own, q_got), jnp.where(first, q_got, q_own)])

    slice_width = out_weight.shape[3]
    out_pair = out_weight.reshape(NC, out_weight.shape[0] // NC, NZ, slice_width)
    out_own = pick(out_pair, c)
    out_got = swap(pick(out_pair, 1 - c))
    out_low = jnp.where(first, out_own, out_got)
    out_high = jnp.where(first, out_got, out_own)
    out_both = jnp.stack([out_low, out_high], axis=2).reshape(-1, NZ * NC * slice_width)
    gain_own = norm_gain.reshape(slice_width)
    gain_got = swap(gain_own)
    gain = jnp.concatenate(
        [jnp.where(first, gain_own, gain_got), jnp.where(first, gain_got, gain_own)]
    )
    head_got = swap(head_weight)

    attn = attend(span_order, xy.reshape(1), chip_queries, packed)
    attn_all = spread(attn, PLANE, planes).reshape(total_rows, -1)

    mixed = jnp.dot(attn_all, out_both, preferred_element_type=F32)
    mine = (jnp.arange(NZ)[:, None] == z) & (jnp.arange(NC)[None, :] == c)
    own_part = jnp.where(
        mine[None, :, :, None],
        residual.reshape(total_rows, 1, 1, slice_width).astype(F32),
        0.0,
    ).reshape(total_rows, -1)
    mixed = mixed + own_part
    mixed_pair = mixed.reshape(planes, NC, q_dev, -1).transpose(1, 0, 2, 3)
    mixed = pick(mixed_pair, c) + swap(pick(mixed_pair, 1 - c))
    width = NC * slice_width
    mixed = rolled(mixed.reshape(half_rows, NZ, width).transpose(1, 0, 2), z)
    hidden = mixed[0] + sum(ring(mixed[k], k) for k in range(1, NZ))

    square_part = jnp.sum(hidden * hidden, axis=1).reshape(-1, 128)
    squares = jnp.sum(spread(square_part, CHIPS, planes * NZ).reshape(planes * NZ, half_rows), axis=0)
    normed = (hidden * lax.rsqrt(squares / D + EPSILON)[:, None] * gain[None, :]).astype(BF16)
    z_rows = half_rows // NZ
    block = spread(normed, PLANE, planes).reshape(planes, NZ, z_rows, width)
    block = jnp.stack(rolled(block.transpose(1, 2, 0, 3), z)).reshape(half_rows, -1)
    block_got = swap(block)

    vocab_width = head_weight.shape[1]

    def summed_logits(weight):
        part = jnp.dot(block, weight, preferred_element_type=F32).astype(F16)
        part = part.reshape(NZ, z_rows, vocab_width)
        return part[0].astype(F32) + sum(ring(part[k], k).astype(F32) for k in range(1, NZ))

    logits = (summed_logits(head_weight), summed_logits(head_got))
    half_targets = pick(targets.reshape(planes, NC, q_dev).transpose(1, 0, 2), c)
    half_targets = jnp.concatenate(rolled(half_targets.reshape(NZ, z_rows), z))
    columns = jnp.arange(vocab_width, dtype=jnp.int32)[None, :]
    hits = tuple(
        columns + (xy * NC + core) * vocab_width == half_targets[:, None] for core in (c, 1 - c)
    )
    grown, stats = [], []
    for hit, part in zip(hits, logits):
        peak = jnp.max(part, axis=1)
        expo = jnp.exp(part - peak[:, None])
        grown.append(expo.astype(BF16))
        stats += [
            peak,
            jnp.sum(expo, axis=1),
            jnp.sum(jnp.where(hit[:z_rows], part, 0.0), axis=1),
        ]
    stats = jnp.pad(jnp.stack(stats), ((0, 2), (0, 128 - z_rows)))
    stats = spread(stats, CHIPS, planes * NZ).reshape(planes, NZ, 8, 128)[:, :, :6, :z_rows]
    stats = stats.reshape(planes, NZ, NC, 3, z_rows)
    row_peak = jnp.max(stats[:, :, :, 0], axis=(0, 2))
    row_total = jnp.sum(
        stats[:, :, :, 1] * jnp.exp(stats[:, :, :, 0] - row_peak[None, :, None]), axis=(0, 2)
    )
    row_lse = row_peak + jnp.log(row_total)
    row_loss = jnp.sum(row_lse - jnp.sum(stats[:, :, :, 2], axis=(0, 2))).reshape(1, 1)
    loss = ((row_loss + swap(row_loss)) / total_rows).reshape(())
    scales = jnp.exp(pick(stats, xy)[:, :, 0] - row_lse[:, None])

    def gathered_grads(part, hit, scale):
        whole = jnp.concatenate([part] + [ring(part, k) for k in range(NZ - 1, 0, -1)])
        scale = jnp.concatenate(rolled(scale, z))
        return (whole.astype(F32) * scale[:, None] - hit.astype(F32)).astype(BF16)

    grad_own, grad_far = (
        gathered_grads(grown[h], hits[h], scales[:, h]) for h in range(NC)
    )
    grad_got = swap(grad_far)
    transposed = (((1,), (1,)), ((), ()))
    grad_rows = lax.dot_general(
        grad_own, head_weight, transposed, preferred_element_type=F32
    ) + lax.dot_general(grad_far, head_got, transposed, preferred_element_type=F32)
    grad_rows = jnp.concatenate(rolled(grad_rows.astype(BF16).reshape(NZ, z_rows, -1), -z))
    grad_parts = exchange(grad_rows, PLANE).reshape(planes, q_dev, -1)
    grad_head = lax.dot_general(
        jnp.concatenate([block, block_got]),
        jnp.concatenate([grad_own, grad_got]),
        (((0,), (0,)), ((), ())),
        preferred_element_type=F32,
    ).astype(BF16)
    grad_parts, grad_head = lax.optimization_barrier((grad_parts, grad_head))
    grad_normed = jnp.sum(grad_parts.astype(F32), axis=0).astype(BF16)
    return (loss, grad_normed, grad_head)


def solution(mesh):
    fine = Mesh(mesh.devices.reshape(NX, NY, NC, NZ), ("x", "y", "c", "z"))
    placed = (
        P(CTX, "z"),
        P(CTX, "z"),
        P(CTX, "z"),
        P(),
        P(),
        P("z", None, CTX, None),
        P(None, "z", CTX, None),
        P("z", CTX, None),
        P("z", CTX),
    )
    return jax.shard_map(
        per_device,
        mesh=fine,
        in_specs=placed,
        out_specs=(P(), P(CTX, "z"), P("z", CTX)),
        check_vma=False,
    )
```
